32 devices in a mesh: chan: 16 (over z, x, core), freq: 2 (over y).
Axes of the slice: x: 2, y: 2, z: 4, core: 2. Of those that a mesh axis runs over, the one named last changes fastest.
Arguments:
- signal: bfloat16 [32, 1024, 2048], P('freq', 'chan'), may hold values from -1000 to 1000
- spatial_taps: float32 [33, 512], replicated, may hold values from -1 to 1
Outputs:
- cross_spectra: bfloat16 [512, 2, 1024, 16], P('freq', None, 'chan')
The draws below stay inside these ranges and needn't reach their ends.
All inputs are finite; a program needn't handle non-finite values.
Results may differ from the reference program's by a relative error of at most 0.0075.
Values may be sent and summed in bfloat16 or wider, within the bound.
A program may use at most 64 MiB of HBM per device.

```python
import math
import jax
import jax.numpy as jnp
from jax import lax

C_DEV = 64
F = 512
NT = 2048
TAPS = 33
SRC_DEV = 1
C = 1024
W = 32
S = 16


def draw_signal(key, part):
    keys = jax.random.split(jax.random.fold_in(key, 17), 3)
    noise = jax.random.normal(keys[0], (W, C, NT + 1), jnp.float32)
    coefficient = 0.8
    top_scale = math.log(10.0)
    colored = noise[:, :, 1:] + coefficient * noise[:, :, :-1]
    channel_scale = jnp.exp(jax.random.uniform(keys[1], (1, C, 1), jnp.float32, 0.0, top_scale))
    window_scale = jnp.exp(jax.random.uniform(keys[2], (W, 1, 1), jnp.float32, 0.0, math.log(10.0)))
    values = jnp.clip(colored * channel_scale * window_scale, -1000.0, 1000.0)
    return values.astype(jnp.bfloat16)


def centred(key, extent, spread, reach, kind=jnp.bfloat16):
    return jnp.clip(spread * jax.random.normal(key, extent, jnp.float32), -reach, reach).astype(kind)


def setup_inputs(seed: int = 0) -> dict:
    key_of = jax.random.split(jax.random.key(seed), 3)
    return {
        "signal": draw_signal(jax.random.fold_in(key_of[2], 71), 0),
        "spatial_taps": centred(key_of[1], (TAPS, F), 0.25, 1.0, jnp.float32),
    }


def fourier_table(samples, bins_total):
    sample_index = jnp.arange(samples, dtype=jnp.int32)
    bin_index = jnp.arange(bins_total, dtype=jnp.int32)
    phase_angle = (sample_index[:, None] * bin_index[None, :] % samples).astype(jnp.float32) * (2.0 * math.pi / samples)
    hann_window = 0.5 - 0.5 * jnp.cos(sample_index.astype(jnp.float32) * (2.0 * math.pi / samples))
    weighting = hann_window[:, None] / math.sqrt(samples)
    stacked = jnp.stack([weighting * jnp.cos(phase_angle), -weighting * jnp.sin(phase_angle)], axis=-1)
    return stacked.reshape(samples, 2 * bins_total).astype(jnp.bfloat16)

def reference(signal, spatial_taps):
    table = fourier_table(NT, F)
    tap_cols = jnp.repeat(spatial_taps, 2, axis=1)
    margin = TAPS // 2

    def per_window(window_rows):
        spectra = jnp.dot(window_rows, table, preferred_element_type=jnp.float32).astype(jnp.bfloat16)
        padded = jnp.concatenate([spectra[C - margin:], spectra, spectra[:margin]], axis=0)
        filtered = jnp.zeros((C, 2 * F), jnp.float32)
        for tap_index in range(TAPS):
            filtered = filtered + tap_cols[tap_index] * padded[tap_index:tap_index + C].astype(jnp.float32)
        mean_power = lax.optimization_barrier(jnp.sum(filtered * filtered, axis=1)) / F
        inverse = 1.0 / jnp.sqrt(mean_power + 1e-06)
        return (filtered * inverse[:, None]).astype(jnp.bfloat16)
    whitened = lax.map(per_window, signal)
    spacing = C_DEV // SRC_DEV
    sources = whitened[:, ::spacing, :]
    block_bins = min(64, F)
    block_count = F // block_bins
    receivers = whitened.reshape(W, C, block_count, block_bins, 2)
    receivers = jnp.transpose(receivers, (2, 0, 1, 3, 4))
    values = sources.reshape(W, S, F, 2)
    rotated = jnp.stack([-values[..., 1], values[..., 0]], axis=-1)
    stacked = jnp.stack([values, rotated], axis=2).reshape(W, S, 2, block_count, block_bins, 2)
    stacked = jnp.transpose(stacked, (3, 0, 1, 2, 4, 5))
    scale = 1.0 / math.sqrt(W)

    def per_block(operands):
        block_recv, block_src = operands
        product = jnp.einsum('wcfp,wskfp->fkcs', block_recv.astype(jnp.float32), block_src.astype(jnp.float32))
        return (product * scale).astype(jnp.bfloat16)
    blocks = lax.map(per_block, (receivers, stacked))
    return blocks.reshape(F, 2, C, S)
```

```python
import functools
import math

import jax
import jax.numpy as jnp
import numpy as np
from jax import lax
from jax.experimental import pallas as pl
from jax.experimental.pallas import tpu as pltpu
from jax.sharding import PartitionSpec as P

SRC_DEV = 1
LANES = 128
FINE = 32
CBLOCK = 16
FBLOCK = 8
XBLOCK = 4
SBLOCK = 16
RUN = 3


def phase_tables(samples, bins_total):
    bins = np.concatenate([np.arange(bins_total), np.ones(LANES, np.int64)])

    def pair(times):
        phase = (times[:, None] * bins[None, :] % samples) * (2.0 * np.pi / samples)
        return np.cos(phase).astype(np.float32), np.sin(phase).astype(np.float32)

    coarse = pair(np.arange(samples // FINE) * FINE)
    fine = pair(np.arange(FINE))
    return coarse + fine


def swap_matrix(outer, inner):
    rows = outer * inner
    row = lax.broadcasted_iota(jnp.int32, (rows, rows), 0)
    col = lax.broadcasted_iota(jnp.int32, (rows, rows), 1)
    wanted = (row % inner) * outer + row // inner
    return (col == wanted).astype(jnp.bfloat16)


def fill_table(cc_ref, cs_ref, fc_ref, fs_ref, table, samples, bins):
    scale = 1.0 / math.sqrt(samples)
    fine_cos = fc_ref[...]
    fine_sin = fs_ref[...]
    half = samples // 2
    lane = lax.broadcasted_iota(jnp.int32, (1, LANES), 1)
    sign = (1 - 2 * lax.rem(lane, 2)).astype(jnp.float32)

    def step(t, carry):
        coarse_cos = cc_ref[pl.ds(t, 1), :]
        coarse_sin = cs_ref[pl.ds(t, 1), :]
        cosine = coarse_cos * fine_cos - coarse_sin * fine_sin
        sine = coarse_sin * fine_cos + coarse_cos * fine_sin
        window = 0.5 * cosine[:, bins:]
        early = (0.5 - window) * scale
        late = (0.5 + window) * scale * sign
        for offset, hann in ((0, early), (half, late)):
            rows = pl.ds(pl.multiple_of(t * FINE + offset, FINE), FINE)
            for start in range(0, bins, LANES):
                table[rows, start : start + LANES] = (
                    hann * cosine[:, start : start + LANES]
                ).astype(jnp.bfloat16)
                table[rows, bins + start : bins + start + LANES] = (
                    -hann * sine[:, start : start + LANES]
                ).astype(jnp.bfloat16)
        return carry

    lax.fori_loop(0, half // FINE, step, 0)


def dft_block(first, signal, table, padded, margin):
    windows, _, samples = signal.shape
    bins = table.shape[1] // 2
    rows = signal[:, pl.ds(first, CBLOCK), :].reshape(windows * CBLOCK, samples)
    swap = swap_matrix(CBLOCK, windows)
    step = min(2 * bins, 512)
    for start in range(0, 2 * bins, step):
        spectra = jnp.dot(
            rows, table[:, start : start + step], preferred_element_type=jnp.float32
        ).astype(jnp.bfloat16)
        swapped = jnp.dot(swap, spectra, preferred_element_type=jnp.float32)
        padded[pl.ds(margin + first, CBLOCK), :, start : start + step] = swapped.astype(
            jnp.bfloat16
        ).reshape(CBLOCK, windows, step)


def filter_block(first, taps_ref, padded, filtered, power, finished):
    taps, bins = taps_ref.shape
    windows = padded.shape[1]
    groups, width = finished.shape[0], finished.shape[4]
    power[...] = jnp.zeros_like(power)

    def tile(f, carry):
        start = pl.multiple_of(f * LANES, LANES)
        lanes = pl.ds(start, LANES)
        weights = [
            jnp.broadcast_to(taps_ref[j : j + 1, lanes], (8, LANES)) for j in range(taps)
        ]
        weights = [
            jnp.concatenate([w] * (windows // 8), axis=0).astype(jnp.bfloat16) for w in weights
        ]
        for part in range(2):
            columns = pl.ds(pl.multiple_of(part * bins + start, LANES), LANES)
            total = [None] * FBLOCK
            short = [None] * FBLOCK
            for row in range(FBLOCK + taps - 1):
                value = padded[first + row, :, columns]
                for o in range(FBLOCK):
                    j = row - o
                    if 0 <= j < taps:
                        term = weights[j] * value
                        short[o] = term if j % RUN == 0 else short[o] + term
                        if j % RUN == RUN - 1 or j == taps - 1:
                            run = short[o].astype(jnp.float32)
                            total[o] = run if total[o] is None else total[o] + run
                    if row - o == taps - 1:
                        filtered[o, :, columns] = total[o]
                        power[o] += total[o] * total[o]
        return carry

    lax.fori_loop(0, bins // LANES, tile, 0)
    mean = jnp.sum(power[...], axis=2, keepdims=True) / bins
    inverse = 1.0 / jnp.sqrt(mean + 1e-06)
    for o in range(FBLOCK):
        for part in range(2):
            for group in range(groups):
                start = part * bins + group * width
                finished[group, part, first + o] = (
                    filtered[o, :, start : start + width] * inverse[o]
                ).astype(jnp.bfloat16)


def prepare_sources(sources, q_ref, qm_ref, qp_ref):
    count, groups, _, windows, width = sources.shape
    block = min(SBLOCK, count)
    swap = swap_matrix(windows, block)
    for s0 in range(0, count, block):

        def one(j, carry):
            halves = []
            for part in range(2):
                rows = sources[s0 : s0 + block, j, part].reshape(block * windows, width)
                halves.append(
                    jnp.dot(swap, rows, preferred_element_type=jnp.float32).reshape(
                        windows, block, width
                    )
                )
            q_ref[j, :, s0 : s0 + block] = halves[0]
            qm_ref[j, :, s0 : s0 + block] = halves[0] - halves[1]
            qp_ref[j, :, s0 : s0 + block] = halves[0] + halves[1]
            return carry

        lax.fori_loop(0, groups, one, 0)


def cross_block(c0, moved, out_ref, a_ref, b_ref, ab_ref, q_ref, qm_ref, qp_ref):
    groups, _, _, windows, width = moved.shape
    count = q_ref.shape[2]
    scale = 1.0 / math.sqrt(groups * windows)
    tile = min(width, LANES)
    block = min(SBLOCK, count)
    for j in range(groups):
        for c in range(XBLOCK):
            real = moved[j, 0, c0 + c].astype(jnp.float32)
            imag = moved[j, 1, c0 + c].astype(jnp.float32)
            a_ref[c, j] = real
            b_ref[c, j] = imag
            ab_ref[c, j] = real + imag
    for s0 in range(0, count, block):
        for start in range(0, width, tile):
            lanes = slice(start, start + tile)

            def windows_of(j, total):
                total = list(total)
                for w in range(windows):
                    q = q_ref[j, w, s0 : s0 + block, lanes]
                    qm = qm_ref[j, w, s0 : s0 + block, lanes]
                    qp = qp_ref[j, w, s0 : s0 + block, lanes]
                    for c in range(XBLOCK):
                        total[3 * c] += ab_ref[c, j, w : w + 1, lanes] * q
                        total[3 * c + 1] += b_ref[c, j, w : w + 1, lanes] * qm
                        total[3 * c + 2] += a_ref[c, j, w : w + 1, lanes] * qp
                return tuple(total)

            zero = jnp.zeros((block, tile), jnp.float32)
            total = lax.fori_loop(0, groups, windows_of, (zero,) * (3 * XBLOCK))
            for c in range(XBLOCK):
                common, second, third = total[3 * c : 3 * c + 3]
                out_ref[0, c0 + c, s0 : s0 + block, lanes] = (
                    (common - second) * scale
                ).astype(jnp.bfloat16)
                out_ref[1, c0 + c, s0 : s0 + block, lanes] = (
                    (common - third) * scale
                ).astype(jnp.bfloat16)


def kernel(
    groups, count, signal_hbm, cc_ref, cs_ref, fc_ref, fs_ref, taps_ref, out_ref,
    signal, table, padded, filtered, power, finished, moved, sources, local,
    a_ref, b_ref, ab_ref, q_ref, qm_ref, qp_ref,
    load_sems, halo_send, halo_recv, y_send, y_recv, own_sems, source_own,
    source_send, source_recv, pair_send, pair_recv, first_send, first_recv,
):
    channels, samples = signal.shape[1:]
    taps, bins = taps_ref.shape
    margin = taps // 2
    half = count // 2
    blocks = channels // CBLOCK
    chunks = channels // FBLOCK
    low_end = margin // FBLOCK
    high_start = chunks - low_end
    chan = lax.axis_index("chan")
    freq = lax.axis_index("freq")
    right = lax.rem(chan + 1, count)
    left = lax.rem(chan + count - 1, count)
    partner = chan + 1 - 2 * lax.rem(chan, 2)

    def to_chan(index):
        return {"chan": index}

    loads = []
    for i in range(blocks):
        span = pl.ds(((i + blocks - 1) % blocks) * CBLOCK, CBLOCK)
        loads.append(
            pltpu.make_async_copy(
                signal_hbm.at[:, span, :], signal.at[:, span, :], load_sems.at[i]
            )
        )
        loads[-1].start()

    barrier = pltpu.get_barrier_semaphore()

    def greet(device):
        pl.semaphore_signal(
            barrier, inc=1, device_id=device, device_id_type=pl.DeviceIdType.MESH
        )

    for device in (left, right, partner):
        greet(to_chan(device))
    for d in range(1, half):
        greet(to_chan(lax.rem(chan + 2 * d, count)))
    for d in range(1, groups):
        greet({"freq": lax.rem(freq + d, groups)})

    fill_table(cc_ref, cs_ref, fc_ref, fs_ref, table, samples, bins)
    pl.semaphore_wait(barrier, 3 + half - 1 + groups - 1)

    def remote(src, dst, send, recv, device):
        return pltpu.make_async_remote_copy(
            src_ref=src, dst_ref=dst, send_sem=send, recv_sem=recv,
            device_id=device, device_id_type=pl.DeviceIdType.MESH,
        )

    low_copy = remote(
        padded.at[pl.ds(channels, margin)], padded.at[pl.ds(0, margin)],
        halo_send.at[0], halo_recv.at[0], to_chan(right),
    )
    high_copy = remote(
        padded.at[pl.ds(margin, margin)], padded.at[pl.ds(margin + channels, margin)],
        halo_send.at[1], halo_recv.at[1], to_chan(left),
    )

    def dft_step(i, carry):
        first = pl.multiple_of(lax.rem(i + blocks - 1, blocks) * CBLOCK, CBLOCK)
        span = pl.ds(first, CBLOCK)
        pltpu.make_async_copy(
            signal_hbm.at[:, span, :], signal.at[:, span, :], load_sems.at[i]
        ).wait()
        dft_block(first, signal, table, padded, margin)

        @pl.when(i == 0)
        def _():
            low_copy.start()

        @pl.when(i == blocks - 1)
        def _():
            high_copy.start()

        return carry

    lax.fori_loop(0, blocks, dft_step, 0)

    def own_copy(k):
        span = pl.ds(k * FBLOCK, FBLOCK)
        return pltpu.make_async_copy(
            finished.at[freq, :, span], moved.at[freq, :, span], own_sems.at[k]
        )

    def y_copy(k, d):
        span = pl.ds(k * FBLOCK, FBLOCK)
        target = lax.rem(freq + d, groups)
        return remote(
            finished.at[target, :, span], moved.at[freq, :, span],
            y_send.at[d - 1, k], y_recv.at[d - 1, k], {"freq": target},
        )

    def compute(k):
        filter_block(k * FBLOCK, taps_ref, padded, filtered, power, finished)

    def send(k):
        for d in range(1, groups):
            y_copy(k, d).start()
        own_copy(k).start()

    def filter_step(k, carry):
        compute(k)
        send(k)
        return carry

    def arrived(k):
        own_copy(k).wait()
        for d in range(1, groups):
            y_copy(k, d).wait_recv()

    def first_copy(d):
        target = lax.rem(freq + d, groups)
        return remote(
            finished.at[target, :, 0], local.at[freq],
            first_send.at[d - 1], first_recv.at[d - 1], {"freq": target},
        )

    ahead = low_end + max(min(3, high_start - low_end), 1)

    def early_step(k, carry):
        compute(k)

        @pl.when(k < ahead - 1)
        def _():
            send(k)

        return carry

    lax.fori_loop(low_end, ahead, early_step, 0)
    low_copy.wait_recv()
    compute(0)
    for d in range(1, groups):
        first_copy(d).start()
    own_first = pltpu.make_async_copy(finished.at[freq, :, 0], local.at[freq], source_own.at[1])
    own_first.start()
    send(ahead - 1)
    send(0)
    lax.fori_loop(ahead, high_start, filter_step, 0)
    own_first.wait()
    for d in range(1, groups):
        first_copy(d).wait_recv()

    mine = local

    def source_copy(d):
        return remote(
            mine, sources.at[chan], source_send.at[d], source_recv.at[d],
            to_chan(lax.rem(chan + 2 * d, count)),
        )

    def pair_copy(d):
        origin = lax.rem(chan + count - 2 * d, count)
        return remote(
            mine if d == 0 else sources.at[origin], sources.at[origin],
            pair_send.at[d], pair_recv.at[d], to_chan(partner),
        )

    for d in range(1, half):
        source_copy(d).start()
    pair_copy(0).start()
    keep = pltpu.make_async_copy(mine, sources.at[chan], source_own.at[0])
    keep.start()

    lax.fori_loop(1, low_end, filter_step, 0)
    high_copy.wait_recv()
    lax.fori_loop(high_start, chunks, filter_step, 0)

    for d in range(1, half):
        source_copy(d).wait_recv()
        pair_copy(d).start()
    keep.wait()
    for d in range(half):
        pair_copy(d).wait_recv()
    prepare_sources(sources, q_ref, qm_ref, qp_ref)

    def cross_step(k, carry):
        arrived(k)

        def inner(i, carry):
            cross_block(
                k * FBLOCK + i * XBLOCK, moved, out_ref,
                a_ref, b_ref, ab_ref, q_ref, qm_ref, qp_ref,
            )
            return carry

        return lax.fori_loop(0, FBLOCK // XBLOCK, inner, carry)

    lax.fori_loop(0, chunks, cross_step, 0)

    low_copy.wait_send()
    high_copy.wait_send()
    for d in range(1, groups):
        first_copy(d).wait_send()
    for d in range(1, half):
        source_copy(d).wait_send()
    for d in range(half):
        pair_copy(d).wait_send()

    def drain(k, carry):
        for d in range(1, groups):
            y_copy(k, d).wait_send()
        return carry

    lax.fori_loop(0, chunks, drain, 0)


def on_device(signal, spatial_taps):
    windows, channels, samples = signal.shape
    taps, bins = spatial_taps.shape
    margin = taps // 2
    groups = lax.axis_size("freq")
    count = lax.axis_size("chan") * SRC_DEV
    width = bins // groups
    chunks = channels // FBLOCK
    tables = [jnp.asarray(t) for t in phase_tables(samples, bins)]
    vmem = pl.BlockSpec(memory_space=pltpu.VMEM)
    dma = pltpu.SemaphoreType.DMA
    rows = pltpu.VMEM((XBLOCK, groups, windows, width), jnp.float32)
    source = pltpu.VMEM((groups, windows, count, width), jnp.float32)
    spectra = pltpu.VMEM((groups, 2, channels, windows, width), jnp.bfloat16)
    result = pl.pallas_call(
        functools.partial(kernel, groups, count),
        in_specs=[pl.BlockSpec(memory_space=pl.ANY)] + [vmem] * 5,
        out_specs=vmem,
        out_shape=pltpu.VMEM((2, channels, count, width), jnp.bfloat16),
        scratch_shapes=[
            pltpu.VMEM(signal.shape, jnp.bfloat16),
            pltpu.VMEM((samples, 2 * bins), jnp.bfloat16),
            pltpu.VMEM((channels + 2 * margin, windows, 2 * bins), jnp.bfloat16),
            pltpu.VMEM((FBLOCK, windows, 2 * bins), jnp.float32),
            pltpu.VMEM((FBLOCK, windows, LANES), jnp.float32),
            spectra,
            spectra,
            pltpu.VMEM((count, groups, 2, windows, width), jnp.bfloat16),
            pltpu.VMEM((groups, 2, windows, width), jnp.bfloat16),
        ]
        + [rows] * 3
        + [source] * 3
        + [
            dma((channels // CBLOCK,)),
            dma((2,)),
            dma((2,)),
            dma((max(groups - 1, 1), chunks)),
            dma((max(groups - 1, 1), chunks)),
            dma((chunks,)),
            dma((2,)),
            dma((count // 2,)),
            dma((count // 2,)),
            dma((count // 2,)),
            dma((count // 2,)),
            dma((max(groups - 1, 1),)),
            dma((max(groups - 1, 1),)),
        ],
        compiler_params=pltpu.CompilerParams(
            collective_id=0, has_side_effects=True, vmem_limit_bytes=60 * 2**20
        ),
    )(signal, *tables, spatial_taps)
    return result.transpose(3, 0, 1, 2)


def solution(mesh):
    placed = (P("freq", "chan", None), P())
    return jax.shard_map(
        on_device,
        mesh=mesh,
        in_specs=placed,
        out_specs=P("freq", None, "chan", None),
        check_vma=False,
    )
```

```python
import functools
import math

import jax
import jax.numpy as jnp
import numpy as np
from jax import lax
from jax.experimental import pallas as pl
from jax.experimental.pallas import tpu as pltpu
from jax.sharding import PartitionSpec as P

SRC_DEV = 1
LANES = 128
FINE = 32
CBLOCK = 16
FBLOCK = 8
XBLOCK = 4
SBLOCK = 16
RUN = 3
PLANE = 4


def phase_tables(samples, bins_total):
    bins = np.concatenate([np.arange(bins_total), np.ones(LANES, np.int64)])

    def pair(times):
        phase = (times[:, None] * bins[None, :] % samples) * (2.0 * np.pi / samples)
        return np.cos(phase).astype(np.float32), np.sin(phase).astype(np.float32)

    coarse = pair(np.arange(samples // FINE) * FINE)
    fine = pair(np.arange(FINE))
    return coarse + fine


def swap_matrix(outer, inner):
    rows = outer * inner
    row = lax.broadcasted_iota(jnp.int32, (rows, rows), 0)
    col = lax.broadcasted_iota(jnp.int32, (rows, rows), 1)
    wanted = (row % inner) * outer + row // inner
    return (col == wanted).astype(jnp.bfloat16)


def fill_table(cc_ref, cs_ref, fc_ref, fs_ref, table, samples, bins):
    scale = 1.0 / math.sqrt(samples)
    fine_cos = fc_ref[...]
    fine_sin = fs_ref[...]
    half = samples // 2
    lane = lax.broadcasted_iota(jnp.int32, (1, LANES), 1)
    sign = (1 - 2 * lax.rem(lane, 2)).astype(jnp.float32)

    def step(t, carry):
        coarse_cos = cc_ref[pl.ds(t, 1), :]
        coarse_sin = cs_ref[pl.ds(t, 1), :]
        cosine = coarse_cos * fine_cos - coarse_sin * fine_sin
        sine = coarse_sin * fine_cos + coarse_cos * fine_sin
        window = 0.5 * cosine[:, bins:]
        early = (0.5 - window) * scale
        late = (0.5 + window) * scale * sign
        for offset, hann in ((0, early), (half, late)):
            rows = pl.ds(pl.multiple_of(t * FINE + offset, FINE), FINE)
            for start in range(0, bins, LANES):
                table[rows, start : start + LANES] = (
                    hann * cosine[:, start : start + LANES]
                ).astype(jnp.bfloat16)
                table[rows, bins + start : bins + start + LANES] = (
                    -hann * sine[:, start : start + LANES]
                ).astype(jnp.bfloat16)
        return carry

    lax.fori_loop(0, half // FINE, step, 0)


def dft_block(first, signal, table, padded, margin):
    windows, _, samples = signal.shape
    bins = table.shape[1] // 2
    rows = signal[:, pl.ds(first, CBLOCK), :].reshape(windows * CBLOCK, samples)
    swap = swap_matrix(CBLOCK, windows)
    step = min(2 * bins, 512)
    for start in range(0, 2 * bins, step):
        spectra = jnp.dot(
            rows, table[:, start : start + step], preferred_element_type=jnp.float32
        ).astype(jnp.bfloat16)
        swapped = jnp.dot(swap, spectra, preferred_element_type=jnp.float32)
        padded[pl.ds(margin + first, CBLOCK), :, start : start + step] = swapped.astype(
            jnp.bfloat16
        ).reshape(CBLOCK, windows, step)


def filter_block(first, taps_ref, padded, filtered, power, finished):
    taps, bins = taps_ref.shape
    windows = padded.shape[1]
    groups, width = finished.shape[0], finished.shape[4]
    power[...] = jnp.zeros_like(power)

    def tile(f, carry):
        start = pl.multiple_of(f * LANES, LANES)
        lanes = pl.ds(start, LANES)
        weights = [
            jnp.broadcast_to(taps_ref[j : j + 1, lanes], (8, LANES)) for j in range(taps)
        ]
        weights = [
            jnp.concatenate([w] * (windows // 8), axis=0).astype(jnp.bfloat16) for w in weights
        ]
        for part in range(2):
            columns = pl.ds(pl.multiple_of(part * bins + start, LANES), LANES)
            total = [None] * FBLOCK
            short = [None] * FBLOCK
            for row in range(FBLOCK + taps - 1):
                value = padded[first + row, :, columns]
                for o in range(FBLOCK):
                    j = row - o
                    if 0 <= j < taps:
                        term = weights[j] * value
                        short[o] = term if j % RUN == 0 else short[o] + term
                        if j % RUN == RUN - 1 or j == taps - 1:
                            run = short[o].astype(jnp.float32)
                            total[o] = run if total[o] is None else total[o] + run
                    if row - o == taps - 1:
                        filtered[o, :, columns] = total[o]
                        power[o] += total[o] * total[o]
        return carry

    lax.fori_loop(0, bins // LANES, tile, 0)
    mean = jnp.sum(power[...], axis=2, keepdims=True) / bins
    inverse = 1.0 / jnp.sqrt(mean + 1e-06)
    for o in range(FBLOCK):
        for part in range(2):
            for group in range(groups):
                start = part * bins + group * width
                finished[group, part, first + o] = (
                    filtered[o, :, start : start + width] * inverse[o]
                ).astype(jnp.bfloat16)


def prepare_sources(sources, q_ref, qm_ref, qp_ref):
    count, groups, _, windows, width = sources.shape
    block = min(SBLOCK, count)
    swap = swap_matrix(windows, block)
    for s0 in range(0, count, block):

        def one(j, carry):
            halves = []
            for part in range(2):
                rows = sources[s0 : s0 + block, j, part].reshape(block * windows, width)
                halves.append(
                    jnp.dot(swap, rows, preferred_element_type=jnp.float32).reshape(
                        windows, block, width
                    )
                )
            q_ref[j, :, s0 : s0 + block] = halves[0]
            qm_ref[j, :, s0 : s0 + block] = halves[0] - halves[1]
            qp_ref[j, :, s0 : s0 + block] = halves[0] + halves[1]
            return carry

        lax.fori_loop(0, groups, one, 0)


def cross_block(c0, moved, out_ref, a_ref, b_ref, ab_ref, q_ref, qm_ref, qp_ref):
    groups, _, _, windows, width = moved.shape
    count = q_ref.shape[2]
    scale = 1.0 / math.sqrt(groups * windows)
    tile = min(width, LANES)
    block = min(SBLOCK, count)
    for j in range(groups):
        for c in range(XBLOCK):
            real = moved[j, 0, c0 + c].astype(jnp.float32)
            imag = moved[j, 1, c0 + c].astype(jnp.float32)
            a_ref[c, j] = real
            b_ref[c, j] = imag
            ab_ref[c, j] = real + imag
    for s0 in range(0, count, block):
        for start in range(0, width, tile):
            lanes = slice(start, start + tile)

            def windows_of(j, total):
                total = list(total)
                for w in range(windows):
                    q = q_ref[j, w, s0 : s0 + block, lanes]
                    qm = qm_ref[j, w, s0 : s0 + block, lanes]
                    qp = qp_ref[j, w, s0 : s0 + block, lanes]
                    for c in range(XBLOCK):
                        total[3 * c] += ab_ref[c, j, w : w + 1, lanes] * q
                        total[3 * c + 1] += b_ref[c, j, w : w + 1, lanes] * qm
                        total[3 * c + 2] += a_ref[c, j, w : w + 1, lanes] * qp
                return tuple(total)

            zero = jnp.zeros((block, tile), jnp.float32)
            total = lax.fori_loop(0, groups, windows_of, (zero,) * (3 * XBLOCK))
            for c in range(XBLOCK):
                common, second, third = total[3 * c : 3 * c + 3]
                out_ref[0, c0 + c, s0 : s0 + block, lanes] = (
                    (common - second) * scale
                ).astype(jnp.bfloat16)
                out_ref[1, c0 + c, s0 : s0 + block, lanes] = (
                    (common - third) * scale
                ).astype(jnp.bfloat16)


def kernel(
    groups, count, signal_hbm, cc_ref, cs_ref, fc_ref, fs_ref, taps_ref, out_ref,
    signal, table, padded, filtered, power, finished, moved, sources, local,
    a_ref, b_ref, ab_ref, q_ref, qm_ref, qp_ref,
    load_sems, halo_send, halo_recv, y_send, y_recv, own_sems, source_own,
    source_send, source_recv, pair_send, pair_recv, first_send, first_recv,
    up_sem, down_sem,
):
    channels, samples = signal.shape[1:]
    taps, bins = taps_ref.shape
    margin = taps // 2
    half = count // 2
    blocks = channels // CBLOCK
    chunks = channels // FBLOCK
    low_end = margin // FBLOCK
    high_start = chunks - low_end
    chan = lax.axis_index("chan")
    freq = lax.axis_index("freq")
    right = lax.rem(chan + 1, count)
    left = lax.rem(chan + count - 1, count)
    partner = chan + 1 - 2 * lax.rem(chan, 2)

    def to_chan(index):
        return {"chan": index}

    loads = []
    for i in range(blocks):
        span = pl.ds(((i + blocks - 1) % blocks) * CBLOCK, CBLOCK)
        loads.append(
            pltpu.make_async_copy(
                signal_hbm.at[:, span, :], signal.at[:, span, :], load_sems.at[i]
            )
        )
        loads[-1].start()

    barrier = pltpu.get_barrier_semaphore()

    def greet(device):
        pl.semaphore_signal(
            barrier, inc=1, device_id=device, device_id_type=pl.DeviceIdType.MESH
        )

    place = lax.rem(chan, PLANE)
    level = chan // PLANE
    levels = count // PLANE

    def when(condition, body):
        pl.when(condition)(body)

    for d in range(1, PLANE):
        greet(to_chan(chan - place + lax.rem(place + d, PLANE)))
    for d in range(1, groups):
        greet({"freq": lax.rem(freq + d, groups)})
    above = level < levels - 1
    below = level > 0
    crossing_up = jnp.logical_and(above, place == PLANE - 1)
    crossing_down = jnp.logical_and(below, place == 0)
    when(above, lambda: greet(to_chan(chan + PLANE)))
    when(below, lambda: greet(to_chan(chan - PLANE)))
    when(crossing_up, lambda: greet(to_chan(chan + 1)))
    when(crossing_down, lambda: greet(to_chan(chan - 1)))
    near = PLANE - 1 + groups - 1
    for condition in (above, below, crossing_up, crossing_down):
        near = near + condition.astype(jnp.int32)

    def tell(sem, device):
        pl.semaphore_signal(
            sem, inc=1, device_id=to_chan(device), device_id_type=pl.DeviceIdType.MESH
        )

    def relay(i):
        def up():
            pl.semaphore_wait(up_sem, 1)
            when(above, lambda: tell(up_sem, chan + PLANE))

        def down():
            pl.semaphore_wait(down_sem, 1)
            when(below, lambda: tell(down_sem, chan - PLANE))

        when(jnp.logical_and(below, i == 0), up)
        turn = jnp.minimum(levels - 2 - level, blocks - 2)
        when(jnp.logical_and(above, i == turn), down)

    fill_table(cc_ref, cs_ref, fc_ref, fs_ref, table, samples, bins)
    pl.semaphore_wait(barrier, near)
    when(jnp.logical_not(below), lambda: when(above, lambda: tell(up_sem, chan + PLANE)))
    when(jnp.logical_not(above), lambda: when(below, lambda: tell(down_sem, chan - PLANE)))

    def remote(src, dst, send, recv, device):
        return pltpu.make_async_remote_copy(
            src_ref=src, dst_ref=dst, send_sem=send, recv_sem=recv,
            device_id=device, device_id_type=pl.DeviceIdType.MESH,
        )

    low_copy = remote(
        padded.at[pl.ds(channels, margin)], padded.at[pl.ds(0, margin)],
        halo_send.at[0], halo_recv.at[0], to_chan(right),
    )
    high_copy = remote(
        padded.at[pl.ds(margin, margin)], padded.at[pl.ds(margin + channels, margin)],
        halo_send.at[1], halo_recv.at[1], to_chan(left),
    )

    def dft_step(i, carry):
        first = pl.multiple_of(lax.rem(i + blocks - 1, blocks) * CBLOCK, CBLOCK)
        span = pl.ds(first, CBLOCK)
        pltpu.make_async_copy(
            signal_hbm.at[:, span, :], signal.at[:, span, :], load_sems.at[i]
        ).wait()
        dft_block(first, signal, table, padded, margin)
        relay(i)

        @pl.when(i == 0)
        def _():
            low_copy.start()

        @pl.when(i == blocks - 1)
        def _():
            high_copy.start()

        return carry

    lax.fori_loop(0, blocks, dft_step, 0)

    def own_copy(k):
        span = pl.ds(k * FBLOCK, FBLOCK)
        return pltpu.make_async_copy(
            finished.at[freq, :, span], moved.at[freq, :, span], own_sems.at[k]
        )

    def y_copy(k, d):
        span = pl.ds(k * FBLOCK, FBLOCK)
        target = lax.rem(freq + d, groups)
        return remote(
            finished.at[target, :, span], moved.at[freq, :, span],
            y_send.at[d - 1, k], y_recv.at[d - 1, k], {"freq": target},
        )

    def compute(k):
        filter_block(k * FBLOCK, taps_ref, padded, filtered, power, finished)

    def send(k):
        for d in range(1, groups):
            y_copy(k, d).start()
        own_copy(k).start()

    def filter_step(k, carry):
        compute(k)
        send(k)
        return carry

    def arrived(k):
        own_copy(k).wait()
        for d in range(1, groups):
            y_copy(k, d).wait_recv()

    def first_copy(d):
        target = lax.rem(freq + d, groups)
        return remote(
            finished.at[target, :, 0], local.at[freq],
            first_send.at[d - 1], first_recv.at[d - 1], {"freq": target},
        )

    ahead = low_end + max(min(3, high_start - low_end), 1)

    def early_step(k, carry):
        compute(k)

        @pl.when(k < ahead - 1)
        def _():
            send(k)

        return carry

    lax.fori_loop(low_end, ahead, early_step, 0)
    low_copy.wait_recv()
    compute(0)
    for d in range(1, groups):
        first_copy(d).start()
    own_first = pltpu.make_async_copy(finished.at[freq, :, 0], local.at[freq], source_own.at[1])
    own_first.start()
    send(ahead - 1)
    send(0)
    lax.fori_loop(ahead, high_start, filter_step, 0)
    own_first.wait()
    for d in range(1, groups):
        first_copy(d).wait_recv()

    mine = local

    def source_copy(d):
        return remote(
            mine, sources.at[chan], source_send.at[d], source_recv.at[d],
            to_chan(lax.rem(chan + 2 * d, count)),
        )

    def pair_copy(d):
        origin = lax.rem(chan + count - 2 * d, count)
        return remote(
            mine if d == 0 else sources.at[origin], sources.at[origin],
            pair_send.at[d], pair_recv.at[d], to_chan(partner),
        )

    for d in range(1, half):
        source_copy(d).start()
    pair_copy(0).start()
    keep = pltpu.make_async_copy(mine, sources.at[chan], source_own.at[0])
    keep.start()

    lax.fori_loop(1, low_end, filter_step, 0)
    high_copy.wait_recv()
    lax.fori_loop(high_start, chunks, filter_step, 0)

    for d in range(1, half):
        source_copy(d).wait_recv()
        pair_copy(d).start()
    keep.wait()
    for d in range(half):
        pair_copy(d).wait_recv()
    prepare_sources(sources, q_ref, qm_ref, qp_ref)

    def cross_step(k, carry):
        arrived(k)

        def inner(i, carry):
            cross_block(
                k * FBLOCK + i * XBLOCK, moved, out_ref,
                a_ref, b_ref, ab_ref, q_ref, qm_ref, qp_ref,
            )
            return carry

        return lax.fori_loop(0, FBLOCK // XBLOCK, inner, carry)

    lax.fori_loop(0, chunks, cross_step, 0)

    low_copy.wait_send()
    high_copy.wait_send()
    for d in range(1, groups):
        first_copy(d).wait_send()
    for d in range(1, half):
        source_copy(d).wait_send()
    for d in range(half):
        pair_copy(d).wait_send()

    def drain(k, carry):
        for d in range(1, groups):
            y_copy(k, d).wait_send()
        return carry

    lax.fori_loop(0, chunks, drain, 0)


def on_device(signal, spatial_taps):
    windows, channels, samples = signal.shape
    taps, bins = spatial_taps.shape
    margin = taps // 2
    groups = lax.axis_size("freq")
    count = lax.axis_size("chan") * SRC_DEV
    width = bins // groups
    chunks = channels // FBLOCK
    tables = [jnp.asarray(t) for t in phase_tables(samples, bins)]
    vmem = pl.BlockSpec(memory_space=pltpu.VMEM)
    dma = pltpu.SemaphoreType.DMA
    rows = pltpu.VMEM((XBLOCK, groups, windows, width), jnp.float32)
    source = pltpu.VMEM((groups, windows, count, width), jnp.float32)
    spectra = pltpu.VMEM((groups, 2, channels, windows, width), jnp.bfloat16)
    result = pl.pallas_call(
        functools.partial(kernel, groups, count),
        in_specs=[pl.BlockSpec(memory_space=pl.ANY)] + [vmem] * 5,
        out_specs=vmem,
        out_shape=pltpu.VMEM((2, channels, count, width), jnp.bfloat16),
        scratch_shapes=[
            pltpu.VMEM(signal.shape, jnp.bfloat16),
            pltpu.VMEM((samples, 2 * bins), jnp.bfloat16),
            pltpu.VMEM((channels + 2 * margin, windows, 2 * bins), jnp.bfloat16),
            pltpu.VMEM((FBLOCK, windows, 2 * bins), jnp.float32),
            pltpu.VMEM((FBLOCK, windows, LANES), jnp.float32),
            spectra,
            spectra,
            pltpu.VMEM((count, groups, 2, windows, width), jnp.bfloat16),
            pltpu.VMEM((groups, 2, windows, width), jnp.bfloat16),
        ]
        + [rows] * 3
        + [source] * 3
        + [
            dma((channels // CBLOCK,)),
            dma((2,)),
            dma((2,)),
            dma((max(groups - 1, 1), chunks)),
            dma((max(groups - 1, 1), chunks)),
            dma((chunks,)),
            dma((2,)),
            dma((count // 2,)),
            dma((count // 2,)),
            dma((count // 2,)),
            dma((count // 2,)),
            dma((max(groups - 1, 1),)),
            dma((max(groups - 1, 1),)),
            pltpu.SemaphoreType.REGULAR,
            pltpu.SemaphoreType.REGULAR,
        ],
        compiler_params=pltpu.CompilerParams(
            collective_id=0, has_side_effects=True, vmem_limit_bytes=60 * 2**20
        ),
    )(signal, *tables, spatial_taps)
    return result.transpose(3, 0, 1, 2)


def solution(mesh):
    placed = (P("freq", "chan", None), P())
    return jax.shard_map(
        on_device,
        mesh=mesh,
        in_specs=placed,
        out_specs=P("freq", None, "chan", None),
        check_vma=False,
    )
```

```python
import functools
import math

import jax
import jax.numpy as jnp
import numpy as np
from jax import lax
from jax.experimental import pallas as pl
from jax.experimental.pallas import tpu as pltpu
from jax.sharding import PartitionSpec as P

SRC_DEV = 1
LANES = 128
FINE = 32
CBLOCK = 16
FBLOCK = 8
XBLOCK = 4
SBLOCK = 16
RUN = 3
PLANE = 4


def phase_tables(samples, bins_total):
    bins = np.concatenate([np.arange(bins_total), np.ones(LANES, np.int64)])

    def pair(times):
        phase = (times[:, None] * bins[None, :] % samples) * (2.0 * np.pi / samples)
        return np.cos(phase).astype(np.float32), np.sin(phase).astype(np.float32)

    coarse = pair(np.arange(samples // FINE) * FINE)
    fine = pair(np.arange(FINE))
    return coarse + fine


def swap_matrix(outer, inner):
    rows = outer * inner
    row = lax.broadcasted_iota(jnp.int32, (rows, rows), 0)
    col = lax.broadcasted_iota(jnp.int32, (rows, rows), 1)
    wanted = (row % inner) * outer + row // inner
    return (col == wanted).astype(jnp.bfloat16)


def fill_table(cc_ref, cs_ref, fc_ref, fs_ref, table, samples, bins):
    scale = 1.0 / math.sqrt(samples)
    fine_cos = fc_ref[...]
    fine_sin = fs_ref[...]
    half = samples // 2
    lane = lax.broadcasted_iota(jnp.int32, (1, LANES), 1)
    sign = (1 - 2 * lax.rem(lane, 2)).astype(jnp.float32)

    def step(t, carry):
        coarse_cos = cc_ref[pl.ds(t, 1), :]
        coarse_sin = cs_ref[pl.ds(t, 1), :]
        cosine = coarse_cos * fine_cos - coarse_sin * fine_sin
        sine = coarse_sin * fine_cos + coarse_cos * fine_sin
        window = 0.5 * cosine[:, bins:]
        early = (0.5 - window) * scale
        late = (0.5 + window) * scale * sign
        for offset, hann in ((0, early), (half, late)):
            rows = pl.ds(pl.multiple_of(t * FINE + offset, FINE), FINE)
            for start in range(0, bins, LANES):
                table[rows, start : start + LANES] = (
                    hann * cosine[:, start : start + LANES]
                ).astype(jnp.bfloat16)
                table[rows, bins + start : bins + start + LANES] = (
                    -hann * sine[:, start : start + LANES]
                ).astype(jnp.bfloat16)
        return carry

    lax.fori_loop(0, half // FINE, step, 0)


def dft_block(first, signal, table, padded, margin):
    windows, _, samples = signal.shape
    bins = table.shape[1] // 2
    rows = signal[:, pl.ds(first, CBLOCK), :].reshape(windows * CBLOCK, samples)
    swap = swap_matrix(CBLOCK, windows)
    step = min(2 * bins, 512)
    for start in range(0, 2 * bins, step):
        spectra = jnp.dot(
            rows, table[:, start : start + step], preferred_element_type=jnp.float32
        ).astype(jnp.bfloat16)
        swapped = jnp.dot(swap, spectra, preferred_element_type=jnp.float32)
        padded[pl.ds(margin + first, CBLOCK), :, start : start + step] = swapped.astype(
            jnp.bfloat16
        ).reshape(CBLOCK, windows, step)


def filter_block(first, taps_ref, padded, filtered, power, finished):
    taps, bins = taps_ref.shape
    windows = padded.shape[1]
    groups, width = finished.shape[0], finished.shape[4]
    power[...] = jnp.zeros_like(power)

    def tile(f, carry):
        start = pl.multiple_of(f * LANES, LANES)
        lanes = pl.ds(start, LANES)
        weights = [
            jnp.broadcast_to(taps_ref[j : j + 1, lanes], (8, LANES)) for j in range(taps)
        ]
        weights = [
            jnp.concatenate([w] * (windows // 8), axis=0).astype(jnp.bfloat16) for w in weights
        ]
        for part in range(2):
            columns = pl.ds(pl.multiple_of(part * bins + start, LANES), LANES)
            total = [None] * FBLOCK
            short = [None] * FBLOCK
            for row in range(FBLOCK + taps - 1):
                value = padded[first + row, :, columns]
                for o in range(FBLOCK):
                    j = row - o
                    if 0 <= j < taps:
                        term = weights[j] * value
                        short[o] = term if j % RUN == 0 else short[o] + term
                        if j % RUN == RUN - 1 or j == taps - 1:
                            run = short[o].astype(jnp.float32)
                            total[o] = run if total[o] is None else total[o] + run
                    if row - o == taps - 1:
                        filtered[o, :, columns] = total[o]
                        power[o] += total[o] * total[o]
        return carry

    lax.fori_loop(0, bins // LANES, tile, 0)
    mean = jnp.sum(power[...], axis=2, keepdims=True) / bins
    inverse = 1.0 / jnp.sqrt(mean + 1e-06)
    for o in range(FBLOCK):
        for part in range(2):
            for group in range(groups):
                start = part * bins + group * width
                finished[group, part, first + o] = (
                    filtered[o, :, start : start + width] * inverse[o]
                ).astype(jnp.bfloat16)


def prepare_sources(sources, q_ref, qm_ref, qp_ref):
    count, groups, _, windows, width = sources.shape
    block = min(SBLOCK, count)
    swap = swap_matrix(windows, block)
    for s0 in range(0, count, block):

        def one(j, carry):
            halves = []
            for part in range(2):
                rows = sources[s0 : s0 + block, j, part].reshape(block * windows, width)
                halves.append(
                    jnp.dot(swap, rows, preferred_element_type=jnp.float32).reshape(
                        windows, block, width
                    )
                )
            q_ref[j, :, s0 : s0 + block] = halves[0]
            qm_ref[j, :, s0 : s0 + block] = halves[0] - halves[1]
            qp_ref[j, :, s0 : s0 + block] = halves[0] + halves[1]
            return carry

        lax.fori_loop(0, groups, one, 0)


def cross_block(c0, moved, out_ref, a_ref, b_ref, ab_ref, q_ref, qm_ref, qp_ref):
    groups, _, _, windows, width = moved.shape
    count = q_ref.shape[2]
    scale = 1.0 / math.sqrt(groups * windows)
    tile = min(width, LANES)
    block = min(SBLOCK, count)
    for j in range(groups):
        for c in range(XBLOCK):
            real = moved[j, 0, c0 + c].astype(jnp.float32)
            imag = moved[j, 1, c0 + c].astype(jnp.float32)
            a_ref[c, j] = real
            b_ref[c, j] = imag
            ab_ref[c, j] = real + imag
    for s0 in range(0, count, block):
        for start in range(0, width, tile):
            lanes = slice(start, start + tile)

            def windows_of(j, total):
                total = list(total)
                for w in range(windows):
                    q = q_ref[j, w, s0 : s0 + block, lanes]
                    qm = qm_ref[j, w, s0 : s0 + block, lanes]
                    qp = qp_ref[j, w, s0 : s0 + block, lanes]
                    for c in range(XBLOCK):
                        total[3 * c] += ab_ref[c, j, w : w + 1, lanes] * q
                        total[3 * c + 1] += b_ref[c, j, w : w + 1, lanes] * qm
                        total[3 * c + 2] += a_ref[c, j, w : w + 1, lanes] * qp
                return tuple(total)

            zero = jnp.zeros((block, tile), jnp.float32)
            total = lax.fori_loop(0, groups, windows_of, (zero,) * (3 * XBLOCK))
            for c in range(XBLOCK):
                common, second, third = total[3 * c : 3 * c + 3]
                out_ref[0, c0 + c, s0 : s0 + block, lanes] = (
                    (common - second) * scale
                ).astype(jnp.bfloat16)
                out_ref[1, c0 + c, s0 : s0 + block, lanes] = (
                    (common - third) * scale
                ).astype(jnp.bfloat16)


def kernel(
    groups, count, signal_hbm, cc_ref, cs_ref, fc_ref, fs_ref, taps_ref, out_ref,
    signal, table, padded, filtered, power, finished, moved, sources, local,
    a_ref, b_ref, ab_ref, q_ref, qm_ref, qp_ref,
    load_sems, halo_send, halo_recv, y_send, y_recv, own_sems, source_own,
    source_send, source_recv, pair_send, pair_recv, first_send, first_recv,
    up_sem, down_sem,
):
    channels, samples = signal.shape[1:]
    taps, bins = taps_ref.shape
    margin = taps // 2
    half = count // 2
    blocks = channels // CBLOCK
    chunks = channels // FBLOCK
    low_end = margin // FBLOCK
    high_start = chunks - low_end
    chan = lax.axis_index("chan")
    freq = lax.axis_index("freq")
    right = lax.rem(chan + 1, count)
    left = lax.rem(chan + count - 1, count)
    partner = chan + 1 - 2 * lax.rem(chan, 2)

    def to_chan(index):
        return {"chan": index}

    loads = []
    for i in range(blocks):
        span = pl.ds((blocks - 1 - i) * CBLOCK, CBLOCK)
        loads.append(
            pltpu.make_async_copy(
                signal_hbm.at[:, span, :], signal.at[:, span, :], load_sems.at[i]
            )
        )
        loads[-1].start()

    barrier = pltpu.get_barrier_semaphore()

    def greet(device):
        pl.semaphore_signal(
            barrier, inc=1, device_id=device, device_id_type=pl.DeviceIdType.MESH
        )

    place = lax.rem(chan, PLANE)
    level = chan // PLANE
    levels = count // PLANE

    def when(condition, body):
        pl.when(condition)(body)

    for d in range(1, PLANE):
        greet(to_chan(chan - place + lax.rem(place + d, PLANE)))
    for d in range(1, groups):
        greet({"freq": lax.rem(freq + d, groups)})
    above = level < levels - 1
    below = level > 0
    crossing_up = jnp.logical_and(above, place == PLANE - 1)
    crossing_down = jnp.logical_and(below, place == 0)
    when(above, lambda: greet(to_chan(chan + PLANE)))
    when(below, lambda: greet(to_chan(chan - PLANE)))
    when(crossing_up, lambda: greet(to_chan(chan + 1)))
    when(crossing_down, lambda: greet(to_chan(chan - 1)))
    near = PLANE - 1 + groups - 1
    for condition in (above, below, crossing_up, crossing_down):
        near = near + condition.astype(jnp.int32)

    def tell(sem, device):
        pl.semaphore_signal(
            sem, inc=1, device_id=to_chan(device), device_id_type=pl.DeviceIdType.MESH
        )

    def relay(i):
        def up():
            pl.semaphore_wait(up_sem, 1)
            when(above, lambda: tell(up_sem, chan + PLANE))

        def down():
            pl.semaphore_wait(down_sem, 1)
            tell(down_sem, chan - PLANE)

        when(jnp.logical_and(below, i == 0), up)
        turn = jnp.minimum(levels - 2 - level, blocks - 2)
        when(jnp.logical_and(jnp.logical_and(above, below), i == turn), down)

    fill_table(cc_ref, cs_ref, fc_ref, fs_ref, table, samples, bins)
    pl.semaphore_wait(barrier, near)
    when(jnp.logical_not(below), lambda: when(above, lambda: tell(up_sem, chan + PLANE)))
    when(jnp.logical_not(above), lambda: when(below, lambda: tell(down_sem, chan - PLANE)))

    def remote(src, dst, send, recv, device):
        return pltpu.make_async_remote_copy(
            src_ref=src, dst_ref=dst, send_sem=send, recv_sem=recv,
            device_id=device, device_id_type=pl.DeviceIdType.MESH,
        )

    low_copy = remote(
        padded.at[pl.ds(channels, margin)], padded.at[pl.ds(0, margin)],
        halo_send.at[0], halo_recv.at[0], to_chan(right),
    )
    high_copy = remote(
        padded.at[pl.ds(margin, margin)], padded.at[pl.ds(margin + channels, margin)],
        halo_send.at[1], halo_recv.at[1], to_chan(left),
    )

    def own_copy(k):
        span = pl.ds(k * FBLOCK, FBLOCK)
        return pltpu.make_async_copy(
            finished.at[freq, :, span], moved.at[freq, :, span], own_sems.at[k]
        )

    def y_copy(k, d):
        span = pl.ds(k * FBLOCK, FBLOCK)
        target = lax.rem(freq + d, groups)
        return remote(
            finished.at[target, :, span], moved.at[freq, :, span],
            y_send.at[d - 1, k], y_recv.at[d - 1, k], {"freq": target},
        )

    def compute(k):
        filter_block(k * FBLOCK, taps_ref, padded, filtered, power, finished)

    def send(k):
        for d in range(1, groups):
            y_copy(k, d).start()
        own_copy(k).start()

    def filter_step(k, carry):
        compute(k)
        send(k)
        return carry

    def arrived(k):
        own_copy(k).wait()
        for d in range(1, groups):
            y_copy(k, d).wait_recv()

    def first_copy(d):
        target = lax.rem(freq + d, groups)
        return remote(
            finished.at[target, :, 0], local.at[freq],
            first_send.at[d - 1], first_recv.at[d - 1], {"freq": target},
        )

    lead = (CBLOCK + margin) // FBLOCK

    def dft_step(i, carry):
        first = pl.multiple_of((blocks - 1 - i) * CBLOCK, CBLOCK)
        span = pl.ds(first, CBLOCK)

        @pl.when(i == blocks - 1)
        def _():
            compute(lead)
            send(lead)

        pltpu.make_async_copy(
            signal_hbm.at[:, span, :], signal.at[:, span, :], load_sems.at[i]
        ).wait()
        dft_block(first, signal, table, padded, margin)
        relay(i)

        @pl.when(i == 0)
        def _():
            low_copy.start()

        @pl.when(jnp.logical_and(i == blocks - 1, chan != 0))
        def _():
            high_copy.start()

        return carry

    lax.fori_loop(0, blocks, dft_step, 0)
    lax.fori_loop(lead + 1, high_start, filter_step, 0)
    compute(low_end)
    when(jnp.logical_and(above, level == 0), lambda: pl.semaphore_wait(down_sem, 1))

    @pl.when(chan == 0)
    def _():
        high_copy.start()

    low_copy.wait_recv()
    compute(0)
    for d in range(1, groups):
        first_copy(d).start()
    own_first = pltpu.make_async_copy(finished.at[freq, :, 0], local.at[freq], source_own.at[1])
    own_first.start()
    send(low_end)
    send(0)
    lax.fori_loop(low_end + 1, lead, filter_step, 0)
    own_first.wait()
    for d in range(1, groups):
        first_copy(d).wait_recv()

    mine = local

    def source_copy(d):
        return remote(
            mine, sources.at[chan], source_send.at[d], source_recv.at[d],
            to_chan(lax.rem(chan + 2 * d, count)),
        )

    def pair_copy(d):
        origin = lax.rem(chan + count - 2 * d, count)
        return remote(
            mine if d == 0 else sources.at[origin], sources.at[origin],
            pair_send.at[d], pair_recv.at[d], to_chan(partner),
        )

    for d in range(1, half):
        source_copy(d).start()
    pair_copy(0).start()
    keep = pltpu.make_async_copy(mine, sources.at[chan], source_own.at[0])
    keep.start()

    lax.fori_loop(1, low_end, filter_step, 0)
    high_copy.wait_recv()
    lax.fori_loop(high_start, chunks, filter_step, 0)

    for d in range(1, half):
        source_copy(d).wait_recv()
        pair_copy(d).start()
    keep.wait()
    for d in range(half):
        pair_copy(d).wait_recv()
    prepare_sources(sources, q_ref, qm_ref, qp_ref)

    def cross_step(k, carry):
        arrived(k)

        def inner(i, carry):
            cross_block(
                k * FBLOCK + i * XBLOCK, moved, out_ref,
                a_ref, b_ref, ab_ref, q_ref, qm_ref, qp_ref,
            )
            return carry

        return lax.fori_loop(0, FBLOCK // XBLOCK, inner, carry)

    lax.fori_loop(0, chunks, cross_step, 0)

    low_copy.wait_send()
    high_copy.wait_send()
    for d in range(1, groups):
        first_copy(d).wait_send()
    for d in range(1, half):
        source_copy(d).wait_send()
    for d in range(half):
        pair_copy(d).wait_send()

    def drain(k, carry):
        for d in range(1, groups):
            y_copy(k, d).wait_send()
        return carry

    lax.fori_loop(0, chunks, drain, 0)


def on_device(signal, spatial_taps):
    windows, channels, samples = signal.shape
    taps, bins = spatial_taps.shape
    margin = taps // 2
    groups = lax.axis_size("freq")
    count = lax.axis_size("chan") * SRC_DEV
    width = bins // groups
    chunks = channels // FBLOCK
    tables = [jnp.asarray(t) for t in phase_tables(samples, bins)]
    vmem = pl.BlockSpec(memory_space=pltpu.VMEM)
    dma = pltpu.SemaphoreType.DMA
    rows = pltpu.VMEM((XBLOCK, groups, windows, width), jnp.float32)
    source = pltpu.VMEM((groups, windows, count, width), jnp.float32)
    spectra = pltpu.VMEM((groups, 2, channels, windows, width), jnp.bfloat16)
    result = pl.pallas_call(
        functools.partial(kernel, groups, count),
        in_specs=[pl.BlockSpec(memory_space=pl.ANY)] + [vmem] * 5,
        out_specs=vmem,
        out_shape=pltpu.VMEM((2, channels, count, width), jnp.bfloat16),
        scratch_shapes=[
            pltpu.VMEM(signal.shape, jnp.bfloat16),
            pltpu.VMEM((samples, 2 * bins), jnp.bfloat16),
            pltpu.VMEM((channels + 2 * margin, windows, 2 * bins), jnp.bfloat16),
            pltpu.VMEM((FBLOCK, windows, 2 * bins), jnp.float32),
            pltpu.VMEM((FBLOCK, windows, LANES), jnp.float32),
            spectra,
            spectra,
            pltpu.VMEM((count, groups, 2, windows, width), jnp.bfloat16),
            pltpu.VMEM((groups, 2, windows, width), jnp.bfloat16),
        ]
        + [rows] * 3
        + [source] * 3
        + [
            dma((channels // CBLOCK,)),
            dma((2,)),
            dma((2,)),
            dma((max(groups - 1, 1), chunks)),
            dma((max(groups - 1, 1), chunks)),
            dma((chunks,)),
            dma((2,)),
            dma((count // 2,)),
            dma((count // 2,)),
            dma((count // 2,)),
            dma((count // 2,)),
            dma((max(groups - 1, 1),)),
            dma((max(groups - 1, 1),)),
            pltpu.SemaphoreType.REGULAR,
            pltpu.SemaphoreType.REGULAR,
        ],
        compiler_params=pltpu.CompilerParams(
            collective_id=0, has_side_effects=True, vmem_limit_bytes=60 * 2**20
        ),
    )(signal, *tables, spatial_taps)
    return result.transpose(3, 0, 1, 2)


def solution(mesh):
    placed = (P("freq", "chan", None), P())
    return jax.shard_map(
        on_device,
        mesh=mesh,
        in_specs=placed,
        out_specs=P("freq", None, "chan", None),
        check_vma=False,
    )
```

```python
import functools
import math

import jax
import jax.numpy as jnp
import numpy as np
from jax import lax
from jax.experimental import pallas as pl
from jax.experimental.pallas import tpu as pltpu
from jax.sharding import PartitionSpec as P

SRC_DEV = 1
LANES = 128
FINE = 32
CBLOCK = 16
FBLOCK = 8
XBLOCK = 4
SBLOCK = 16
RUN = 3
PLANE = 4


def phase_tables(samples, bins_total):
    bins = np.concatenate([np.arange(bins_total), np.ones(LANES, np.int64)])

    def pair(times):
        phase = (times[:, None] * bins[None, :] % samples) * (2.0 * np.pi / samples)
        return np.cos(phase).astype(np.float32), np.sin(phase).astype(np.float32)

    coarse = pair(np.arange(samples // FINE) * FINE)
    fine = pair(np.arange(FINE))
    return coarse + fine


def swap_matrix(outer, inner):
    rows = outer * inner
    row = lax.broadcasted_iota(jnp.int32, (rows, rows), 0)
    col = lax.broadcasted_iota(jnp.int32, (rows, rows), 1)
    wanted = (row % inner) * outer + row // inner
    return (col == wanted).astype(jnp.bfloat16)


def fill_table(cc_ref, cs_ref, fc_ref, fs_ref, table, samples, bins):
    scale = 1.0 / math.sqrt(samples)
    fine_cos = fc_ref[...]
    fine_sin = fs_ref[...]
    half = samples // 2
    lane = lax.broadcasted_iota(jnp.int32, (1, LANES), 1)
    sign = (1 - 2 * lax.rem(lane, 2)).astype(jnp.float32)

    def step(t, carry):
        coarse_cos = cc_ref[pl.ds(t, 1), :]
        coarse_sin = cs_ref[pl.ds(t, 1), :]
        cosine = coarse_cos * fine_cos - coarse_sin * fine_sin
        sine = coarse_sin * fine_cos + coarse_cos * fine_sin
        window = 0.5 * cosine[:, bins:]
        early = (0.5 - window) * scale
        late = (0.5 + window) * scale * sign
        for offset, hann in ((0, early), (half, late)):
            rows = pl.ds(pl.multiple_of(t * FINE + offset, FINE), FINE)
            for start in range(0, bins, LANES):
                table[rows, start : start + LANES] = (
                    hann * cosine[:, start : start + LANES]
                ).astype(jnp.bfloat16)
                table[rows, bins + start : bins + start + LANES] = (
                    -hann * sine[:, start : start + LANES]
                ).astype(jnp.bfloat16)
        return carry

    lax.fori_loop(0, half // FINE, step, 0)


def dft_block(first, signal, table, padded, margin):
    windows, _, samples = signal.shape
    bins = table.shape[1] // 2
    rows = signal[:, pl.ds(first, CBLOCK), :].reshape(windows * CBLOCK, samples)
    swap = swap_matrix(CBLOCK, windows)
    step = min(2 * bins, 512)
    for start in range(0, 2 * bins, step):
        spectra = jnp.dot(
            rows, table[:, start : start + step], preferred_element_type=jnp.float32
        ).astype(jnp.bfloat16)
        swapped = jnp.dot(swap, spectra, preferred_element_type=jnp.float32)
        padded[pl.ds(margin + first, CBLOCK), :, start : start + step] = swapped.astype(
            jnp.bfloat16
        ).reshape(CBLOCK, windows, step)


def filter_block(first, taps_ref, padded, filtered, power, finished):
    taps, bins = taps_ref.shape
    windows = padded.shape[1]
    groups, width = finished.shape[0], finished.shape[4]
    power[...] = jnp.zeros_like(power)

    def tile(f, carry):
        start = pl.multiple_of(f * LANES, LANES)
        lanes = pl.ds(start, LANES)
        weights = [
            jnp.broadcast_to(taps_ref[j : j + 1, lanes], (8, LANES)) for j in range(taps)
        ]
        weights = [
            jnp.concatenate([w] * (windows // 8), axis=0).astype(jnp.bfloat16) for w in weights
        ]
        for part in range(2):
            columns = pl.ds(pl.multiple_of(part * bins + start, LANES), LANES)
            total = [None] * FBLOCK
            short = [None] * FBLOCK
            for row in range(FBLOCK + taps - 1):
                value = padded[first + row, :, columns]
                for o in range(FBLOCK):
                    j = row - o
                    if 0 <= j < taps:
                        term = weights[j] * value
                        short[o] = term if j % RUN == 0 else short[o] + term
                        if j % RUN == RUN - 1 or j == taps - 1:
                            run = short[o].astype(jnp.float32)
                            total[o] = run if total[o] is None else total[o] + run
                    if row - o == taps - 1:
                        filtered[o, :, columns] = total[o]
                        power[o] += total[o] * total[o]
        return carry

    lax.fori_loop(0, bins // LANES, tile, 0)
    mean = jnp.sum(power[...], axis=2, keepdims=True) / bins
    inverse = 1.0 / jnp.sqrt(mean + 1e-06)
    for o in range(FBLOCK):
        for part in range(2):
            for group in range(groups):
                start = part * bins + group * width
                finished[group, part, first + o] = (
                    filtered[o, :, start : start + width] * inverse[o]
                ).astype(jnp.bfloat16)


def prepare_sources(sources, q_ref, qm_ref, qp_ref):
    count, groups, _, windows, width = sources.shape
    block = min(SBLOCK, count)
    swap = swap_matrix(windows, block)
    for s0 in range(0, count, block):

        def one(j, carry):
            halves = []
            for part in range(2):
                rows = sources[s0 : s0 + block, j, part].reshape(block * windows, width)
                halves.append(
                    jnp.dot(swap, rows, preferred_element_type=jnp.float32).reshape(
                        windows, block, width
                    )
                )
            q_ref[j, :, s0 : s0 + block] = halves[0]
            qm_ref[j, :, s0 : s0 + block] = halves[0] - halves[1]
            qp_ref[j, :, s0 : s0 + block] = halves[0] + halves[1]
            return carry

        lax.fori_loop(0, groups, one, 0)


def cross_block(c0, moved, out_ref, a_ref, b_ref, ab_ref, q_ref, qm_ref, qp_ref):
    groups, _, _, windows, width = moved.shape
    count = q_ref.shape[2]
    scale = 1.0 / math.sqrt(groups * windows)
    tile = min(width, LANES)
    block = min(SBLOCK, count)
    for j in range(groups):
        for c in range(XBLOCK):
            real = moved[j, 0, c0 + c].astype(jnp.float32)
            imag = moved[j, 1, c0 + c].astype(jnp.float32)
            a_ref[c, j] = real
            b_ref[c, j] = imag
            ab_ref[c, j] = real + imag
    for s0 in range(0, count, block):
        for start in range(0, width, tile):
            lanes = slice(start, start + tile)

            def windows_of(j, total):
                total = list(total)
                for w in range(windows):
                    q = q_ref[j, w, s0 : s0 + block, lanes]
                    qm = qm_ref[j, w, s0 : s0 + block, lanes]
                    qp = qp_ref[j, w, s0 : s0 + block, lanes]
                    for c in range(XBLOCK):
                        total[3 * c] += ab_ref[c, j, w : w + 1, lanes] * q
                        total[3 * c + 1] += b_ref[c, j, w : w + 1, lanes] * qm
                        total[3 * c + 2] += a_ref[c, j, w : w + 1, lanes] * qp
                return tuple(total)

            zero = jnp.zeros((block, tile), jnp.float32)
            total = lax.fori_loop(0, groups, windows_of, (zero,) * (3 * XBLOCK))
            for c in range(XBLOCK):
                common, second, third = total[3 * c : 3 * c + 3]
                out_ref[0, c0 + c, s0 : s0 + block, lanes] = (
                    (common - second) * scale
                ).astype(jnp.bfloat16)
                out_ref[1, c0 + c, s0 : s0 + block, lanes] = (
                    (common - third) * scale
                ).astype(jnp.bfloat16)


def kernel(
    groups, count, signal_hbm, cc_ref, cs_ref, fc_ref, fs_ref, taps_ref, out_ref,
    signal, table, padded, filtered, power, finished, moved, sources, local,
    a_ref, b_ref, ab_ref, q_ref, qm_ref, qp_ref,
    load_sems, halo_send, halo_recv, y_send, y_recv, own_sems, source_own,
    source_send, source_recv, pair_send, pair_recv, first_send, first_recv,
    up_sem, down_sem,
):
    channels, samples = signal.shape[1:]
    taps, bins = taps_ref.shape
    margin = taps // 2
    half = count // 2
    blocks = channels // CBLOCK
    chunks = channels // FBLOCK
    low_end = margin // FBLOCK
    high_start = chunks - low_end
    chan = lax.axis_index("chan")
    freq = lax.axis_index("freq")
    right = lax.rem(chan + 1, count)
    left = lax.rem(chan + count - 1, count)
    partner = chan + 1 - 2 * lax.rem(chan, 2)

    def to_chan(index):
        return {"chan": index}

    loads = []
    for i in range(blocks):
        span = pl.ds((blocks - 1 - i) * CBLOCK, CBLOCK)
        loads.append(
            pltpu.make_async_copy(
                signal_hbm.at[:, span, :], signal.at[:, span, :], load_sems.at[i]
            )
        )
        loads[-1].start()

    barrier = pltpu.get_barrier_semaphore()

    def greet(device):
        pl.semaphore_signal(
            barrier, inc=1, device_id=device, device_id_type=pl.DeviceIdType.MESH
        )

    place = lax.rem(chan, PLANE)
    level = chan // PLANE
    levels = count // PLANE

    def when(condition, body):
        pl.when(condition)(body)

    for d in range(1, PLANE):
        greet(to_chan(chan - place + lax.rem(place + d, PLANE)))
    for d in range(1, groups):
        greet({"freq": lax.rem(freq + d, groups)})
    above = level < levels - 1
    below = level > 0
    crossing_up = jnp.logical_and(above, place == PLANE - 1)
    crossing_down = jnp.logical_and(below, place == 0)
    when(above, lambda: greet(to_chan(chan + PLANE)))
    when(below, lambda: greet(to_chan(chan - PLANE)))
    when(crossing_up, lambda: greet(to_chan(chan + 1)))
    when(crossing_down, lambda: greet(to_chan(chan - 1)))
    near = PLANE - 1 + groups - 1
    for condition in (above, below, crossing_up, crossing_down):
        near = near + condition.astype(jnp.int32)

    def tell(sem, device):
        pl.semaphore_signal(
            sem, inc=1, device_id=to_chan(device), device_id_type=pl.DeviceIdType.MESH
        )

    def relay(i):
        def up():
            pl.semaphore_wait(up_sem, 1)
            when(above, lambda: tell(up_sem, chan + PLANE))

        def down():
            pl.semaphore_wait(down_sem, 1)
            tell(down_sem, chan - PLANE)

        when(jnp.logical_and(below, i == 0), up)
        turn = jnp.minimum(levels - 2 - level, blocks - 2)
        when(jnp.logical_and(jnp.logical_and(above, below), i == turn), down)

    fill_table(cc_ref, cs_ref, fc_ref, fs_ref, table, samples, bins)
    pl.semaphore_wait(barrier, near)
    when(jnp.logical_not(below), lambda: when(above, lambda: tell(up_sem, chan + PLANE)))
    when(jnp.logical_not(above), lambda: when(below, lambda: tell(down_sem, chan - PLANE)))

    def remote(src, dst, send, recv, device):
        return pltpu.make_async_remote_copy(
            src_ref=src, dst_ref=dst, send_sem=send, recv_sem=recv,
            device_id=device, device_id_type=pl.DeviceIdType.MESH,
        )

    low_copy = remote(
        padded.at[pl.ds(channels, margin)], padded.at[pl.ds(0, margin)],
        halo_send.at[0], halo_recv.at[0], to_chan(right),
    )
    high_copy = remote(
        padded.at[pl.ds(margin, margin)], padded.at[pl.ds(margin + channels, margin)],
        halo_send.at[1], halo_recv.at[1], to_chan(left),
    )

    def own_copy(k):
        span = pl.ds(k * FBLOCK, FBLOCK)
        return pltpu.make_async_copy(
            finished.at[freq, :, span], moved.at[freq, :, span], own_sems.at[k]
        )

    def y_copy(k, d):
        span = pl.ds(k * FBLOCK, FBLOCK)
        target = lax.rem(freq + d, groups)
        return remote(
            finished.at[target, :, span], moved.at[freq, :, span],
            y_send.at[d - 1, k], y_recv.at[d - 1, k], {"freq": target},
        )

    def compute(k):
        filter_block(k * FBLOCK, taps_ref, padded, filtered, power, finished)

    def send(k):
        for d in range(1, groups):
            y_copy(k, d).start()
        own_copy(k).start()

    def filter_step(k, carry):
        compute(k)
        send(k)
        return carry

    def arrived(k):
        own_copy(k).wait()
        for d in range(1, groups):
            y_copy(k, d).wait_recv()

    def first_copy(d):
        target = lax.rem(freq + d, groups)
        return remote(
            finished.at[target, :, 0], local.at[freq],
            first_send.at[d - 1], first_recv.at[d - 1], {"freq": target},
        )

    lead = (CBLOCK + margin) // FBLOCK

    def dft_step(i, carry):
        first = pl.multiple_of((blocks - 1 - i) * CBLOCK, CBLOCK)
        span = pl.ds(first, CBLOCK)

        @pl.when(i == blocks - 1)
        def _():
            compute(lead)
            send(lead)

        pltpu.make_async_copy(
            signal_hbm.at[:, span, :], signal.at[:, span, :], load_sems.at[i]
        ).wait()
        dft_block(first, signal, table, padded, margin)
        relay(i)

        @pl.when(i == 0)
        def _():
            low_copy.start()

        @pl.when(jnp.logical_and(i == blocks - 1, chan != 0))
        def _():
            high_copy.start()

        return carry

    lax.fori_loop(0, blocks, dft_step, 0)
    lax.fori_loop(lead + 1, high_start, filter_step, 0)
    compute(low_end)
    when(jnp.logical_and(above, level == 0), lambda: pl.semaphore_wait(down_sem, 1))

    @pl.when(chan == 0)
    def _():
        high_copy.start()

    wrapped = chan == 0
    split = jnp.where(wrapped, lead, low_end + 1)
    when(wrapped, lambda: send(low_end))
    lax.fori_loop(low_end + 1, split, filter_step, 0)
    low_copy.wait_recv()
    compute(0)
    for d in range(1, groups):
        first_copy(d).start()
    own_first = pltpu.make_async_copy(finished.at[freq, :, 0], local.at[freq], source_own.at[1])
    own_first.start()
    when(jnp.logical_not(wrapped), lambda: send(low_end))
    send(0)
    lax.fori_loop(split, lead, filter_step, 0)
    own_first.wait()
    for d in range(1, groups):
        first_copy(d).wait_recv()

    mine = local

    def source_copy(d):
        return remote(
            mine, sources.at[chan], source_send.at[d], source_recv.at[d],
            to_chan(lax.rem(chan + 2 * d, count)),
        )

    def pair_copy(d):
        origin = lax.rem(chan + count - 2 * d, count)
        return remote(
            mine if d == 0 else sources.at[origin], sources.at[origin],
            pair_send.at[d], pair_recv.at[d], to_chan(partner),
        )

    for d in range(1, half):
        source_copy(d).start()
    pair_copy(0).start()
    keep = pltpu.make_async_copy(mine, sources.at[chan], source_own.at[0])
    keep.start()

    lax.fori_loop(1, low_end, filter_step, 0)
    high_copy.wait_recv()
    lax.fori_loop(high_start, chunks, filter_step, 0)

    for d in range(1, half):
        source_copy(d).wait_recv()
        pair_copy(d).start()
    keep.wait()
    for d in range(half):
        pair_copy(d).wait_recv()
    prepare_sources(sources, q_ref, qm_ref, qp_ref)

    def cross_step(k, carry):
        arrived(k)

        def inner(i, carry):
            cross_block(
                k * FBLOCK + i * XBLOCK, moved, out_ref,
                a_ref, b_ref, ab_ref, q_ref, qm_ref, qp_ref,
            )
            return carry

        return lax.fori_loop(0, FBLOCK // XBLOCK, inner, carry)

    lax.fori_loop(0, chunks, cross_step, 0)

    low_copy.wait_send()
    high_copy.wait_send()
    for d in range(1, groups):
        first_copy(d).wait_send()
    for d in range(1, half):
        source_copy(d).wait_send()
    for d in range(half):
        pair_copy(d).wait_send()

    def drain(k, carry):
        for d in range(1, groups):
            y_copy(k, d).wait_send()
        return carry

    lax.fori_loop(0, chunks, drain, 0)


def on_device(signal, spatial_taps):
    windows, channels, samples = signal.shape
    taps, bins = spatial_taps.shape
    margin = taps // 2
    groups = lax.axis_size("freq")
    count = lax.axis_size("chan") * SRC_DEV
    width = bins // groups
    chunks = channels // FBLOCK
    tables = [jnp.asarray(t) for t in phase_tables(samples, bins)]
    vmem = pl.BlockSpec(memory_space=pltpu.VMEM)
    dma = pltpu.SemaphoreType.DMA
    rows = pltpu.VMEM((XBLOCK, groups, windows, width), jnp.float32)
    source = pltpu.VMEM((groups, windows, count, width), jnp.float32)
    spectra = pltpu.VMEM((groups, 2, channels, windows, width), jnp.bfloat16)
    result = pl.pallas_call(
        functools.partial(kernel, groups, count),
        in_specs=[pl.BlockSpec(memory_space=pl.ANY)] + [vmem] * 5,
        out_specs=vmem,
        out_shape=pltpu.VMEM((2, channels, count, width), jnp.bfloat16),
        scratch_shapes=[
            pltpu.VMEM(signal.shape, jnp.bfloat16),
            pltpu.VMEM((samples, 2 * bins), jnp.bfloat16),
            pltpu.VMEM((channels + 2 * margin, windows, 2 * bins), jnp.bfloat16),
            pltpu.VMEM((FBLOCK, windows, 2 * bins), jnp.float32),
            pltpu.VMEM((FBLOCK, windows, LANES), jnp.float32),
            spectra,
            spectra,
            pltpu.VMEM((count, groups, 2, windows, width), jnp.bfloat16),
            pltpu.VMEM((groups, 2, windows, width), jnp.bfloat16),
        ]
        + [rows] * 3
        + [source] * 3
        + [
            dma((channels // CBLOCK,)),
            dma((2,)),
            dma((2,)),
            dma((max(groups - 1, 1), chunks)),
            dma((max(groups - 1, 1), chunks)),
            dma((chunks,)),
            dma((2,)),
            dma((count // 2,)),
            dma((count // 2,)),
            dma((count // 2,)),
            dma((count // 2,)),
            dma((max(groups - 1, 1),)),
            dma((max(groups - 1, 1),)),
            pltpu.SemaphoreType.REGULAR,
            pltpu.SemaphoreType.REGULAR,
        ],
        compiler_params=pltpu.CompilerParams(
            collective_id=0, has_side_effects=True, vmem_limit_bytes=60 * 2**20
        ),
    )(signal, *tables, spatial_taps)
    return result.transpose(3, 0, 1, 2)


def solution(mesh):
    placed = (P("freq", "chan", None), P())
    return jax.shard_map(
        on_device,
        mesh=mesh,
        in_specs=placed,
        out_specs=P("freq", None, "chan", None),
        check_vma=False,
    )
```
